32 devices in a mesh: row: 16 (over z, y, x), col: 2 (over core).
Axes of the slice: x: 2, y: 2, z: 4, core: 2. Of those that a mesh axis runs over, the one named last changes fastest.
Arguments:
- pencil_left: bfloat16 [4, 16, 256, 4, 2, 256], P(None, 'row', None, None, 'col'), may hold values from -0.09375 to 0.09375
- pencil_right: bfloat16 [4, 16, 256, 4, 2, 256], P(None, 'row', None, None, 'col'), may hold values from -0.09375 to 0.09375
- basis_panel: bfloat16 [4, 16, 256, 4, 2, 256], P(None, 'row', None, None, 'col'), may hold values from -0.125 to 0.125
- block_inverses: float32 [4, 2, 256, 256], replicated, may hold values from -0.2 to 2.3
- pencil_shift: float32 [], replicated, may hold values from 0.5 to 1.5
- start_vectors: float32 [4, 16, 256, 512], P(None, 'row', None, 'col'), may hold values from -6 to 6
Outputs:
- pending: float32 [4, 16, 256, 512], P(None, 'row', None, 'col')
- image: float32 [4, 16, 256, 512], P(None, 'row', None, 'col')
The draws below stay inside these ranges and needn't reach their ends.
All inputs are finite; a program needn't handle non-finite values.
Results may differ from the reference program's by a relative error of at most 0.0043.
Values may be sent and summed in bfloat16 or wider, within the bound.
A program may use at most 64 MiB of HBM per device.

```python
import math
import jax
import jax.numpy as jnp
from jax import lax

ORDER = 16384
NB = 256
STEPS = 8
NEV = 512
RB = 4
PB = 4
N_ROW = 16
N_COL = 2


def draw_block_inverses(key, part):
    first_key, second_key = jax.random.split(jax.random.fold_in(key, 17))
    scales = jnp.exp(jax.random.uniform(first_key, (PB, N_COL, NB), jnp.float32, -0.7, 0.7))
    spread = jnp.clip(jax.random.normal(second_key, (PB, N_COL, NB, NB), jnp.float32), -5.0, 5.0)
    spread = jnp.clip(spread * (0.6 / math.sqrt(NB)), -0.19, 0.19)
    identity = jnp.eye(NB, dtype=jnp.float32)
    return identity * scales[..., None] + spread


def steps_of(own_key, dims, shards, low, top_value):
    factor_of = 1.0
    for position, parts in shards:
        draws = jax.random.uniform(jax.random.fold_in(jax.random.fold_in(own_key, 6), position), (parts,), jnp.float32, low / len(shards), top_value / len(shards))
        factor_of = factor_of * jnp.repeat(jnp.exp(draws), dims[position] // parts).reshape((-1,) + (1,) * (len(dims) - 1 - position))
    return factor_of


def normal_values(rng, shape, width, most, pieces=(), kind=jnp.bfloat16):
    level = steps_of(rng, shape, pieces, -0.22, 0.18) if pieces else 1.0
    array = jax.random.normal(rng, shape, jnp.float32) * width * level
    return jnp.minimum(jnp.maximum(array, -most), most).astype(kind)


def setup_inputs(seed: int = 0) -> dict:
    key_of = jax.random.split(jax.random.key(seed), 7)
    return {
        "pencil_left": normal_values(key_of[0], (RB, N_ROW, NB, PB, N_COL, NB), (2 * STEPS * NB) ** -0.5, 0.09375, ((1, 16), (4, 2))),
        "pencil_right": normal_values(key_of[1], (RB, N_ROW, NB, PB, N_COL, NB), (2 * STEPS * NB) ** -0.5, 0.09375, ((1, 16), (4, 2))),
        "basis_panel": normal_values(key_of[2], (RB, N_ROW, NB, PB, N_COL, NB), (STEPS * NB) ** -0.5, 0.125, ((1, 16), (4, 2))),
        "block_inverses": draw_block_inverses(jax.random.fold_in(key_of[6], 71), 0),
        "pencil_shift": jnp.clip(jax.random.uniform(key_of[4], (), jnp.float32, 0.5, 1.5), 0.5, 1.5),
        "start_vectors": normal_values(key_of[5], (RB, N_ROW, NB, NEV), 1.0, 6.0, ((1, 16), (3, 2)), jnp.float32),
    }


def reference(pencil_left, pencil_right, basis_panel, block_inverses, pencil_shift, start_vectors):
    panel_width = STEPS * NB
    left_whole = pencil_left.reshape(ORDER, panel_width)
    right_whole = pencil_right.reshape(ORDER, panel_width)
    basis_whole = basis_panel.reshape(ORDER, panel_width)
    inverse_blocks = block_inverses.reshape(STEPS, NB, NB)
    pending = start_vectors.reshape(ORDER, NEV).astype(jnp.float32)
    first_block = ORDER // NB - STEPS
    row_blocks = jnp.arange(ORDER // NB, dtype=jnp.int32)
    solved = []
    for column in range(STEPS - 1, -1, -1):
        target = first_block + column
        block_rhs = pending[target * NB:(target + 1) * NB]
        vectors = jnp.dot(inverse_blocks[column], block_rhs, precision=lax.Precision.HIGHEST).astype(jnp.bfloat16)
        solved.append(vectors)
        left_cols = left_whole[:, column * NB:(column + 1) * NB]
        right_cols = right_whole[:, column * NB:(column + 1) * NB]
        update = jnp.dot(left_cols, vectors, preferred_element_type=jnp.float32) - pencil_shift * jnp.dot(right_cols, vectors, preferred_element_type=jnp.float32)
        above = (row_blocks < target)[:, None, None]
        update = jnp.where(above, update.reshape(ORDER // NB, NB, NEV), jnp.float32(0.0)).reshape(ORDER, NEV)
        pending = pending - update
    solved_all = jnp.concatenate(solved[::-1], axis=0)
    image = jnp.dot(basis_whole, solved_all, preferred_element_type=jnp.float32)
    return pending.reshape(RB, N_ROW, NB, NEV), image.reshape(RB, N_ROW, NB, NEV)
```

```python
import functools

import jax
import jax.numpy as jnp
from jax import lax
from jax.experimental import pallas as pl
from jax.experimental.pallas import tpu as pltpu
from jax.sharding import PartitionSpec as P

MESH = pl.DeviceIdType.MESH
CHUNKS = 2
LAG = 1


def bit_of(value, place):
    return (value // (1 << place)) % 2


def flip(value, place):
    return value + (1 - 2 * bit_of(value, place)) * (1 << place)


def kernel(rows, shift_ref, left_hbm, right_hbm, basis_hbm, inverse_hbm, start_hbm,
           pend_ref, image_ref, left, right, basis, inverse, solved,
           start_sem, inverse_sem, top_sem, bulk_sem, top_send, bulk_send, solved_sem, solved_send):
    me = lax.axis_index("row")
    core = lax.axis_index("col")
    other = 1 - core
    panel_local, blocks, size, _ = left_hbm.shape
    steps = solved.shape[0]
    width = solved.shape[3]
    bits = rows.bit_length() - 1
    top = blocks - 1
    base = rows - steps
    shift = shift_ref[0]
    is_solver = me >= base
    fed = jnp.logical_and(me >= base - 1, me < rows - 1)

    def start_copy(a):
        return pltpu.make_async_copy(start_hbm.at[a], pend_ref.at[a], start_sem.at[a])

    start_copy(top).start()
    own = jnp.maximum(me - base, 0)
    inverse_copy = pltpu.make_async_copy(inverse_hbm.at[own], inverse, inverse_sem)
    inverse_copy.start()

    barrier = pltpu.get_barrier_semaphore()
    pl.semaphore_signal(barrier, inc=1, device_id=(me, other), device_id_type=MESH)
    for place in range(bits):
        pl.semaphore_signal(barrier, inc=1, device_id=(flip(me, place), core), device_id_type=MESH)

    @pl.when(is_solver)
    def _():
        pl.semaphore_signal(barrier, inc=1, device_id=(me - 1, core), device_id_type=MESH)

    @pl.when(fed)
    def _():
        pl.semaphore_signal(barrier, inc=1, device_id=(me + 1, core), device_id_type=MESH)

    pl.semaphore_wait(barrier, bits + 1 + is_solver.astype(jnp.int32) + fed.astype(jnp.int32))

    sources = ((left_hbm, left), (right_hbm, right), (basis_hbm, basis))

    def top_parts(b, column):
        return [(left_hbm.at[b, top], left.at[column, top], 0), (right_hbm.at[b, top], right.at[column, top], 1)]

    def bulk_parts(b, column):
        found = [(basis_hbm.at[b], basis.at[column], 0)]
        if top > 0:
            found.append((left_hbm.at[b, pl.ds(0, top)], left.at[column, pl.ds(0, top)], 1))
            found.append((right_hbm.at[b, pl.ds(0, top)], right.at[column, pl.ds(0, top)], 2))
        return found

    def local_copy(part, sem, column):
        return pltpu.make_async_copy(part[0], part[1], sem.at[column, part[2]])

    def remote_copy(part, sem, send, b, column):
        return pltpu.make_async_remote_copy(
            src_ref=part[0], dst_ref=part[1], send_sem=send.at[b, part[2]],
            recv_sem=sem.at[column, part[2]], device_id=(me, other), device_id_type=MESH)

    for parts, sem, send in ((top_parts, top_sem, top_send), (bulk_parts, bulk_sem, bulk_send)):
        for b in range(panel_local - 1, -1, -1):
            column = b * 2 + core
            for part in parts(b, column):
                remote_copy(part, sem, send, b, column).start()
                local_copy(part, sem, column).start()
    for a in range(top):
        start_copy(a).start()

    def wait_parts(parts, sem, column):
        for part in parts(0, column):
            pltpu.make_async_copy(part[1], part[1], sem.at[column, part[2]]).wait()

    def send(column, chunk, place, target):
        return pltpu.make_async_remote_copy(
            src_ref=solved.at[column, chunk], dst_ref=solved.at[column, chunk],
            send_sem=solved_send.at[column, chunk, place], recv_sem=solved_sem.at[column, chunk],
            device_id=(target, core), device_id_type=MESH)

    def each_send(column, chunk, act):
        root = base + column
        relative = 0
        for place in range(bits):
            relative = relative + ((bit_of(me, place) + bit_of(root, place)) % 2) * (1 << place)

        @pl.when(me == root)
        def _():
            act(send(column, chunk, bits, me - 1))

        for place in range(bits):
            target = flip(me, place)

            @pl.when(jnp.logical_and(relative < (1 << place), target != root - 1))
            def _():
                act(send(column, chunk, place, target))

    def solve(column, chunk):
        rhs = pend_ref[top, :, chunk * width:(chunk + 1) * width]
        solved[column, chunk] = jnp.dot(
            inverse[...], rhs, precision=lax.Precision.HIGHEST,
            preferred_element_type=jnp.float32).astype(jnp.bfloat16)

    image_ref[...] = jnp.zeros_like(image_ref)
    start_copy(top).wait()
    inverse_copy.wait()

    @pl.when(me == rows - 1)
    def _():
        for chunk in range(CHUNKS):
            solve(steps - 1, chunk)
            each_send(steps - 1, chunk, lambda copy: copy.start())

    for a in range(top):
        start_copy(a).wait()

    def bulk(column):
        wait_parts(bulk_parts, bulk_sem, column)
        block = jnp.concatenate([solved[column, chunk] for chunk in range(CHUNKS)], axis=1)

        def row_block(a, carry):
            image_ref[a] += jnp.dot(basis[column, a], block, preferred_element_type=jnp.float32)
            return carry

        lax.fori_loop(0, blocks, row_block, 0)

        def upper_block(a, carry):
            pend_ref[a] -= (
                jnp.dot(left[column, a], block, preferred_element_type=jnp.float32)
                - shift * jnp.dot(right[column, a], block, preferred_element_type=jnp.float32))
            return carry

        if top > 0:
            lax.fori_loop(0, top, upper_block, 0)

    def turn(t, carry):
        column = steps - 1 - t
        root = base + column
        wait_parts(top_parts, top_sem, column)
        for chunk in range(CHUNKS):
            @pl.when(me != root)
            def _():
                landed = solved.at[column, chunk]
                pltpu.make_async_copy(landed, landed, solved_sem.at[column, chunk]).wait()
                each_send(column, chunk, lambda copy: copy.start())

            @pl.when(me < root)
            def _():
                block = solved[column, chunk]
                here = slice(chunk * width, (chunk + 1) * width)
                pend_ref[top, :, here] -= (
                    jnp.dot(left[column, top], block, preferred_element_type=jnp.float32)
                    - shift * jnp.dot(right[column, top], block, preferred_element_type=jnp.float32))

            @pl.when(jnp.logical_and(me == root - 1, column > 0))
            def _():
                solve(column - 1, chunk)
                each_send(column - 1, chunk, lambda copy: copy.start())

        @pl.when(t >= LAG)
        def _():
            bulk(column + LAG)

        return carry

    lax.fori_loop(0, steps, turn, 0)
    for column in range(LAG - 1, -1, -1):
        bulk(column)

    def drain(column, carry):
        for chunk in range(CHUNKS):
            each_send(column, chunk, lambda copy: copy.wait_send())
        return carry

    lax.fori_loop(0, steps, drain, 0)
    for parts, sem, sent in ((top_parts, top_sem, top_send), (bulk_parts, bulk_sem, bulk_send)):
        for b in range(panel_local):
            column = b * 2 + core
            for part in parts(b, column):
                remote_copy(part, sem, sent, b, column).wait_send()


def local(pencil_left, pencil_right, basis_panel, block_inverses, pencil_shift, start_vectors):
    rows = lax.axis_size("row")
    blocks, _, size, panel_local, _, _ = pencil_left.shape
    slice_width = start_vectors.shape[3]
    steps = block_inverses.shape[0] * block_inverses.shape[1]
    assert rows > steps and rows & (rows - 1) == 0 and lax.axis_size("col") == 2
    bits = rows.bit_length() - 1

    def panel(array):
        return jnp.transpose(array[:, 0, :, :, 0, :], (2, 0, 1, 3))

    any_space = pl.BlockSpec(memory_space=pl.ANY)
    whole = pl.BlockSpec(memory_space=pltpu.VMEM)
    shape_out = jax.ShapeDtypeStruct((blocks, size, slice_width), jnp.float32)
    matrix = pltpu.VMEM((steps, blocks, size, size), jnp.bfloat16)
    dma = pltpu.SemaphoreType.DMA
    pending, image = pl.pallas_call(
        functools.partial(kernel, rows),
        out_shape=(shape_out, shape_out),
        in_specs=[pl.BlockSpec(memory_space=pltpu.SMEM)] + [any_space] * 5,
        out_specs=(whole, whole),
        scratch_shapes=[
            matrix, matrix, matrix,
            pltpu.VMEM((size, size), jnp.float32),
            pltpu.VMEM((steps, CHUNKS, size, slice_width // CHUNKS), jnp.bfloat16),
            dma((blocks,)), dma(()),
            dma((steps, 2)), dma((steps, 3)),
            dma((panel_local, 2)), dma((panel_local, 3)),
            dma((steps, CHUNKS)), dma((steps, CHUNKS, bits + 1)),
        ],
        compiler_params=pltpu.CompilerParams(
            collective_id=0, has_side_effects=True, vmem_limit_bytes=48 * 1024 * 1024),
        name="panel_solve",
    )(
        pencil_shift.reshape(1), panel(pencil_left), panel(pencil_right), panel(basis_panel),
        block_inverses.reshape(steps, size, size), start_vectors[:, 0],
    )
    return pending[:, None], image[:, None]


def solution(mesh):
    in_specs = (
        P(None, "row", None, None, "col", None),
        P(None, "row", None, None, "col", None),
        P(None, "row", None, None, "col", None),
        P(),
        P(),
        P(None, "row", None, "col"),
    )
    out_specs = (P(None, "row", None, "col"), P(None, "row", None, "col"))
    return jax.shard_map(local, mesh=mesh, in_specs=in_specs, out_specs=out_specs, check_vma=False)
```

```python
import functools

import jax
import jax.numpy as jnp
from jax import lax
from jax.experimental import pallas as pl
from jax.experimental.pallas import tpu as pltpu
from jax.sharding import PartitionSpec as P

MESH = pl.DeviceIdType.MESH
CHUNKS = 2


def bit_of(value, place):
    return (value // (1 << place)) % 2


def flip(value, place):
    return value + (1 - 2 * bit_of(value, place)) * (1 << place)


def kernel(rows, pencil_hbm, basis_hbm, inverse_hbm, start_hbm,
           pend_ref, image_ref, pencil, basis, inverse, solved,
           start_sem, inverse_sem, top_sem, bulk_sem, top_send, bulk_send, solved_sem, solved_send):
    me = lax.axis_index("row")
    core = lax.axis_index("col")
    other = 1 - core
    panel_local, blocks, size, _ = pencil_hbm.shape
    steps = solved.shape[0]
    width = solved.shape[3]
    bits = rows.bit_length() - 1
    low = bits - 2
    plane = 1 << low
    layer = me // plane
    top = blocks - 1
    base = rows - steps
    is_solver = me >= base
    fed = jnp.logical_and(me >= base - 1, me < rows - 1)

    def start_copy(a):
        return pltpu.make_async_copy(start_hbm.at[a], pend_ref.at[a], start_sem.at[a])

    start_copy(top).start()
    own = jnp.maximum(me - base, 0)
    inverse_copy = pltpu.make_async_copy(inverse_hbm.at[own], inverse, inverse_sem)
    inverse_copy.start()

    barrier = pltpu.get_barrier_semaphore()
    pl.semaphore_signal(barrier, inc=1, device_id=(me, other), device_id_type=MESH)
    for place in range(low):
        pl.semaphore_signal(barrier, inc=1, device_id=(flip(me, place), core), device_id_type=MESH)

    @pl.when(layer < 3)
    def _():
        pl.semaphore_signal(barrier, inc=1, device_id=(me + plane, core), device_id_type=MESH)

    @pl.when(layer > 0)
    def _():
        pl.semaphore_signal(barrier, inc=1, device_id=(me - plane, core), device_id_type=MESH)

    @pl.when(is_solver)
    def _():
        pl.semaphore_signal(barrier, inc=1, device_id=(me - 1, core), device_id_type=MESH)

    @pl.when(fed)
    def _():
        pl.semaphore_signal(barrier, inc=1, device_id=(me + 1, core), device_id_type=MESH)

    pl.semaphore_wait(barrier, low + 1 + sum(flag.astype(jnp.int32) for flag in (is_solver, fed, layer < 3, layer > 0)))

    def top_parts(b, column):
        return [(pencil_hbm.at[b, top], pencil.at[column, top], 0)]

    def bulk_parts(b, column):
        found = [(basis_hbm.at[b], basis.at[column], 0)]
        if top > 0:
            found.append((pencil_hbm.at[b, pl.ds(0, top)], pencil.at[column, pl.ds(0, top)], 1))
        return found

    def local_copy(part, sem, column):
        return pltpu.make_async_copy(part[0], part[1], sem.at[column, part[2]])

    def remote_copy(part, sem, send, b, column):
        return pltpu.make_async_remote_copy(
            src_ref=part[0], dst_ref=part[1], send_sem=send.at[b, part[2]],
            recv_sem=sem.at[column, part[2]], device_id=(me, other), device_id_type=MESH)

    for parts, sem, send in ((top_parts, top_sem, top_send), (bulk_parts, bulk_sem, bulk_send)):
        for b in range(panel_local - 1, -1, -1):
            column = b * 2 + core
            for part in parts(b, column):
                remote_copy(part, sem, send, b, column).start()
                local_copy(part, sem, column).start()
    for a in range(top):
        start_copy(a).start()

    def wait_parts(parts, sem, column):
        for part in parts(0, column):
            pltpu.make_async_copy(part[1], part[1], sem.at[column, part[2]]).wait()

    def send(column, chunk, place, target):
        return pltpu.make_async_remote_copy(
            src_ref=solved.at[column, chunk], dst_ref=solved.at[column, chunk],
            send_sem=solved_send.at[column, chunk, place], recv_sem=solved_sem.at[column, chunk],
            device_id=(target, core), device_id_type=MESH)

    def tree_send(column, chunk, act):
        root = base + column
        root_layer = root // plane
        relative = sum(((bit_of(me, place) + bit_of(root, place)) % 2) * (1 << place) for place in range(low))

        def edge(place, target, taken):
            @pl.when(jnp.logical_and(taken, target != root - 1))
            def _():
                act(send(column, chunk, place, target))

        in_line = relative == 0
        edge(low, me - plane, in_line & (layer <= root_layer) & (layer > 0))
        edge(low + 1, me + plane, in_line & (layer >= root_layer) & (layer < 3))
        for place in range(low):
            edge(place, flip(me, place), relative < (1 << place))

    def begin(copy):
        copy.start()

    def end(copy):
        copy.wait_send()

    def solve(column, chunk):
        rhs = pend_ref[top, :, chunk * width:(chunk + 1) * width]
        solved[column, chunk] = jnp.dot(
            inverse[...], rhs, precision=lax.Precision.HIGHEST,
            preferred_element_type=jnp.float32).astype(jnp.bfloat16)

    image_ref[...] = jnp.zeros_like(image_ref)
    start_copy(top).wait()
    inverse_copy.wait()

    @pl.when(me == rows - 1)
    def _():
        for chunk in range(CHUNKS):
            solve(steps - 1, chunk)
            begin(send(steps - 1, chunk, bits, me - 1))
        for chunk in range(CHUNKS):
            tree_send(steps - 1, chunk, begin)

    for a in range(top):
        start_copy(a).wait()

    def bulk(*columns):
        vectors = []
        for column in columns:
            wait_parts(bulk_parts, bulk_sem, column)
            vectors.append(jnp.concatenate([solved[column, chunk] for chunk in range(CHUNKS)], axis=1))

        def product(matrix, a):
            return sum(jnp.dot(matrix[column, a], block, preferred_element_type=jnp.float32)
                       for column, block in zip(columns, vectors))

        for a in range(blocks):
            image_ref[a] += product(basis, a)
        for a in range(top):
            pend_ref[a] -= product(pencil, a)

    def turn(t, carry):
        column = steps - 1 - t
        root = base + column
        wait_parts(top_parts, top_sem, column)
        is_next = jnp.logical_and(me == root - 1, column > 0)
        for chunk in range(CHUNKS):
            @pl.when(me != root)
            def _():
                landed = solved.at[column, chunk]
                pltpu.make_async_copy(landed, landed, solved_sem.at[column, chunk]).wait()

            @pl.when(jnp.logical_and(me != root, jnp.logical_not(is_next)))
            def _():
                tree_send(column, chunk, begin)

            @pl.when(me < root)
            def _():
                block = solved[column, chunk]
                here = slice(chunk * width, (chunk + 1) * width)
                pend_ref[top, :, here] -= jnp.dot(pencil[column, top], block, preferred_element_type=jnp.float32)

            @pl.when(is_next)
            def _():
                solve(column - 1, chunk)
                begin(send(column - 1, chunk, bits, me - 1))

        @pl.when(is_next)
        def _():
            for chunk in range(CHUNKS):
                tree_send(column, chunk, begin)
            for chunk in range(CHUNKS):
                tree_send(column - 1, chunk, begin)

        @pl.when(jnp.logical_and(t % 2 == 0, t > 0))
        def _():
            bulk(column + 1, column + 2)

        @pl.when(column == 1)
        def _():
            bulk(column)

        return carry

    lax.fori_loop(0, steps, turn, 0)
    bulk(0)

    def drain(column, carry):
        for chunk in range(CHUNKS):
            tree_send(column, chunk, end)

            @pl.when(me == base + column)
            def _():
                end(send(column, chunk, bits, me - 1))

        return carry

    lax.fori_loop(0, steps, drain, 0)
    for parts, sem, sent in ((top_parts, top_sem, top_send), (bulk_parts, bulk_sem, bulk_send)):
        for b in range(panel_local):
            column = b * 2 + core
            for part in parts(b, column):
                remote_copy(part, sem, sent, b, column).wait_send()


def local(pencil_left, pencil_right, basis_panel, block_inverses, pencil_shift, start_vectors):
    rows = lax.axis_size("row")
    blocks, _, size, panel_local, _, _ = pencil_left.shape
    slice_width = start_vectors.shape[3]
    steps = block_inverses.shape[0] * block_inverses.shape[1]
    assert rows > steps and steps % 2 == 0 and rows >= 8 and rows & (rows - 1) == 0 and lax.axis_size("col") == 2
    bits = rows.bit_length() - 1

    def panel(array):
        return jnp.transpose(array[:, 0, :, :, 0, :], (2, 0, 1, 3))

    combined = (
        pencil_left.astype(jnp.float32) - pencil_shift * pencil_right.astype(jnp.float32)
    ).astype(jnp.bfloat16)
    any_space = pl.BlockSpec(memory_space=pl.ANY)
    whole = pl.BlockSpec(memory_space=pltpu.VMEM)
    shape_out = jax.ShapeDtypeStruct((blocks, size, slice_width), jnp.float32)
    matrix = pltpu.VMEM((steps, blocks, size, size), jnp.bfloat16)
    dma = pltpu.SemaphoreType.DMA
    pending, image = pl.pallas_call(
        functools.partial(kernel, rows),
        out_shape=(shape_out, shape_out),
        in_specs=[any_space] * 4,
        out_specs=(whole, whole),
        scratch_shapes=[
            matrix, matrix,
            pltpu.VMEM((size, size), jnp.float32),
            pltpu.VMEM((steps, CHUNKS, size, slice_width // CHUNKS), jnp.bfloat16),
            dma((blocks,)), dma(()),
            dma((steps, 1)), dma((steps, 2)),
            dma((panel_local, 1)), dma((panel_local, 2)),
            dma((steps, CHUNKS)), dma((steps, CHUNKS, bits + 1)),
        ],
        compiler_params=pltpu.CompilerParams(
            collective_id=0, has_side_effects=True, vmem_limit_bytes=48 * 1024 * 1024),
        name="panel_solve",
    )(
        panel(combined), panel(basis_panel),
        block_inverses.reshape(steps, size, size), start_vectors[:, 0],
    )
    return pending[:, None], image[:, None]


def solution(mesh):
    in_specs = (
        P(None, "row", None, None, "col", None),
        P(None, "row", None, None, "col", None),
        P(None, "row", None, None, "col", None),
        P(),
        P(),
        P(None, "row", None, "col"),
    )
    out_specs = (P(None, "row", None, "col"), P(None, "row", None, "col"))
    return jax.shard_map(local, mesh=mesh, in_specs=in_specs, out_specs=out_specs, check_vma=False)
```

```python
import functools

import jax
import jax.numpy as jnp
from jax import lax
from jax.experimental import pallas as pl
from jax.experimental.pallas import tpu as pltpu
from jax.sharding import PartitionSpec as P

MESH = pl.DeviceIdType.MESH
CHUNKS = 2


def bit_of(value, place):
    return (value // (1 << place)) % 2


def flip(value, place):
    return value + (1 - 2 * bit_of(value, place)) * (1 << place)


def kernel(rows, pencil_hbm, rest_hbm, basis_hbm, inverse_hbm, start_hbm,
           pend_ref, image_ref, pencil, rest, basis, inverse, solved,
           start_sem, inverse_sem, top_sem, bulk_sem, top_send, bulk_send, solved_sem, solved_send):
    me = lax.axis_index("row")
    core = lax.axis_index("col")
    other = 1 - core
    panel_local, blocks, size, _ = pencil_hbm.shape
    steps = solved.shape[0]
    width = solved.shape[3]
    bits = rows.bit_length() - 1
    low = bits - 2
    plane = 1 << low
    layer = me // plane
    top = blocks - 1
    base = rows - steps
    is_solver = me > base
    fed = jnp.logical_and(me >= base, me < rows - 1)

    def start_copy(a):
        return pltpu.make_async_copy(start_hbm.at[a], pend_ref.at[a], start_sem.at[a])

    start_copy(top).start()
    own = jnp.maximum(me - base, 0)
    inverse_copy = pltpu.make_async_copy(inverse_hbm.at[own], inverse, inverse_sem)
    inverse_copy.start()

    barrier = pltpu.get_barrier_semaphore()
    pl.semaphore_signal(barrier, inc=1, device_id=(me, other), device_id_type=MESH)
    for place in range(low):
        pl.semaphore_signal(barrier, inc=1, device_id=(flip(me, place), core), device_id_type=MESH)

    @pl.when(layer < 3)
    def _():
        pl.semaphore_signal(barrier, inc=1, device_id=(me + plane, core), device_id_type=MESH)

    @pl.when(layer > 0)
    def _():
        pl.semaphore_signal(barrier, inc=1, device_id=(me - plane, core), device_id_type=MESH)

    @pl.when(is_solver)
    def _():
        pl.semaphore_signal(barrier, inc=1, device_id=(me - 1, core), device_id_type=MESH)

    @pl.when(fed)
    def _():
        pl.semaphore_signal(barrier, inc=1, device_id=(me + 1, core), device_id_type=MESH)

    pl.semaphore_wait(barrier, low + 1 + sum(flag.astype(jnp.int32) for flag in (is_solver, fed, layer < 3, layer > 0)))

    def top_parts(b, column):
        return [(pencil_hbm.at[b, top], pencil.at[column, top], 0), (rest_hbm.at[b], rest.at[column], 1)]

    def bulk_parts(b, column):
        found = [(basis_hbm.at[b], basis.at[column], 0)]
        if top > 0:
            found.append((pencil_hbm.at[b, pl.ds(0, top)], pencil.at[column, pl.ds(0, top)], 1))
        return found

    def local_copy(part, sem, column):
        return pltpu.make_async_copy(part[0], part[1], sem.at[column, part[2]])

    def remote_copy(part, sem, send, b, column):
        return pltpu.make_async_remote_copy(
            src_ref=part[0], dst_ref=part[1], send_sem=send.at[b, part[2]],
            recv_sem=sem.at[column, part[2]], device_id=(me, other), device_id_type=MESH)

    for parts, sem, send in ((top_parts, top_sem, top_send), (bulk_parts, bulk_sem, bulk_send)):
        for b in range(panel_local - 1, -1, -1):
            column = b * 2 + core
            for part in parts(b, column):
                remote_copy(part, sem, send, b, column).start()
                local_copy(part, sem, column).start()
    for a in range(top):
        start_copy(a).start()

    def wait_parts(parts, sem, column):
        for part in parts(0, column):
            pltpu.make_async_copy(part[1], part[1], sem.at[column, part[2]]).wait()

    def send(column, chunk, place, target):
        return pltpu.make_async_remote_copy(
            src_ref=solved.at[column, chunk], dst_ref=solved.at[column, chunk],
            send_sem=solved_send.at[column, chunk, place], recv_sem=solved_sem.at[column, chunk],
            device_id=(target, core), device_id_type=MESH)

    def tree_send(column, chunk, act):
        root = base + column
        root_layer = root // plane
        relative = sum(((bit_of(me, place) + bit_of(root, place)) % 2) * (1 << place) for place in range(low))

        def edge(place, target, taken):
            @pl.when(taken & ((target != root - 1) | (column == 0)))
            def _():
                act(send(column, chunk, place, target))

        in_line = relative == 0
        edge(low, me - plane, in_line & (layer <= root_layer) & (layer > 0))
        edge(low + 1, me + plane, in_line & (layer >= root_layer) & (layer < 3))
        for place in range(low):
            edge(place, flip(me, place), relative < (1 << place))

    def begin(copy):
        copy.start()

    def end(copy):
        copy.wait_send()

    def solve(column, chunk):
        rhs = pend_ref[top, :, chunk * width:(chunk + 1) * width]
        solved[column, chunk] = jnp.dot(
            inverse[...], rhs, precision=lax.Precision.HIGHEST,
            preferred_element_type=jnp.float32).astype(jnp.bfloat16)

    image_ref[...] = jnp.zeros_like(image_ref)
    start_copy(top).wait()
    inverse_copy.wait()

    @pl.when(me == rows - 1)
    def _():
        for chunk in range(CHUNKS):
            solve(steps - 1, chunk)
            begin(send(steps - 1, chunk, bits, me - 1))
        for chunk in range(CHUNKS):
            tree_send(steps - 1, chunk, begin)

    for a in range(top):
        start_copy(a).wait()

    def bulk(*columns):
        vectors = []
        for column in columns:
            wait_parts(bulk_parts, bulk_sem, column)
            vectors.append(jnp.concatenate([solved[column, chunk] for chunk in range(CHUNKS)], axis=1))

        def product(matrix, a):
            return sum(jnp.dot(matrix[column, a], block, preferred_element_type=jnp.float32)
                       for column, block in zip(columns, vectors))

        for a in range(blocks):
            image_ref[a] += product(basis, a)
        for a in range(top):
            pend_ref[a] -= product(pencil, a)

    def turn(t, carry):
        column = steps - 1 - t
        root = base + column
        wait_parts(top_parts, top_sem, column)
        is_next = jnp.logical_and(me == root - 1, column > 0)
        for chunk in range(CHUNKS):
            @pl.when(me != root)
            def _():
                landed = solved.at[column, chunk]
                pltpu.make_async_copy(landed, landed, solved_sem.at[column, chunk]).wait()

            @pl.when(jnp.logical_and(me != root, jnp.logical_not(is_next)))
            def _():
                tree_send(column, chunk, begin)

            @pl.when(me < root)
            def _():
                block = solved[column, chunk]
                here = slice(chunk * width, (chunk + 1) * width)
                pend_ref[top, :, here] -= (
                    jnp.dot(pencil[column, top], block, preferred_element_type=jnp.float32)
                    + jnp.dot(rest[column], block, preferred_element_type=jnp.float32))

            @pl.when(is_next)
            def _():
                solve(column - 1, chunk)

                @pl.when(column > 1)
                def _():
                    begin(send(column - 1, chunk, bits, me - 1))

        @pl.when(is_next)
        def _():
            for chunk in range(CHUNKS):
                tree_send(column, chunk, begin)
            for chunk in range(CHUNKS):
                tree_send(column - 1, chunk, begin)

        @pl.when(jnp.logical_and(t % 2 == 0, t > 0))
        def _():
            bulk(column + 1, column + 2)

        @pl.when(column == 1)
        def _():
            bulk(column)

        return carry

    lax.fori_loop(0, steps, turn, 0)
    bulk(0)

    def drain(column, carry):
        for chunk in range(CHUNKS):
            tree_send(column, chunk, end)

            @pl.when(jnp.logical_and(me == base + column, column > 0))
            def _():
                end(send(column, chunk, bits, me - 1))

        return carry

    lax.fori_loop(0, steps, drain, 0)
    for parts, sem, sent in ((top_parts, top_sem, top_send), (bulk_parts, bulk_sem, bulk_send)):
        for b in range(panel_local):
            column = b * 2 + core
            for part in parts(b, column):
                remote_copy(part, sem, sent, b, column).wait_send()


def local(pencil_left, pencil_right, basis_panel, block_inverses, pencil_shift, start_vectors):
    rows = lax.axis_size("row")
    blocks, _, size, panel_local, _, _ = pencil_left.shape
    slice_width = start_vectors.shape[3]
    steps = block_inverses.shape[0] * block_inverses.shape[1]
    assert rows > steps and steps % 2 == 0 and rows >= 8 and rows & (rows - 1) == 0 and lax.axis_size("col") == 2
    bits = rows.bit_length() - 1

    def panel(array):
        return jnp.transpose(array[:, 0, :, :, 0, :], (2, 0, 1, 3))

    def difference(left, right):
        exact = left.astype(jnp.float32) - pencil_shift * right.astype(jnp.float32)
        return exact, lax.reduce_precision(exact, 8, 7)

    combined = difference(pencil_left, pencil_right)[1]
    exact, rounded = difference(pencil_left[blocks - 1:], pencil_right[blocks - 1:])
    rest = (exact - rounded).astype(jnp.bfloat16)
    any_space = pl.BlockSpec(memory_space=pl.ANY)
    whole = pl.BlockSpec(memory_space=pltpu.VMEM)
    shape_out = jax.ShapeDtypeStruct((blocks, size, slice_width), jnp.float32)
    matrix = pltpu.VMEM((steps, blocks, size, size), jnp.bfloat16)
    dma = pltpu.SemaphoreType.DMA
    pending, image = pl.pallas_call(
        functools.partial(kernel, rows),
        out_shape=(shape_out, shape_out),
        in_specs=[any_space] * 5,
        out_specs=(whole, whole),
        scratch_shapes=[
            matrix, pltpu.VMEM((steps, size, size), jnp.bfloat16), matrix,
            pltpu.VMEM((size, size), jnp.float32),
            pltpu.VMEM((steps, CHUNKS, size, slice_width // CHUNKS), jnp.bfloat16),
            dma((blocks,)), dma(()),
            dma((steps, 2)), dma((steps, 2)),
            dma((panel_local, 2)), dma((panel_local, 2)),
            dma((steps, CHUNKS)), dma((steps, CHUNKS, bits + 1)),
        ],
        compiler_params=pltpu.CompilerParams(
            collective_id=0, has_side_effects=True, vmem_limit_bytes=48 * 1024 * 1024),
        name="panel_solve",
    )(
        panel(combined.astype(jnp.bfloat16)), panel(rest)[:, 0], panel(basis_panel),
        block_inverses.reshape(steps, size, size), start_vectors[:, 0],
    )
    return pending[:, None], image[:, None]


def solution(mesh):
    in_specs = (
        P(None, "row", None, None, "col", None),
        P(None, "row", None, None, "col", None),
        P(None, "row", None, None, "col", None),
        P(),
        P(),
        P(None, "row", None, "col"),
    )
    out_specs = (P(None, "row", None, "col"), P(None, "row", None, "col"))
    return jax.shard_map(local, mesh=mesh, in_specs=in_specs, out_specs=out_specs, check_vma=False)
```
